32 devices in a mesh: atom: 16 (over z, x, core), energy: 2 (over y).
Axes of the slice: x: 2, y: 2, z: 4, core: 2. Of those that a mesh axis runs over, the one named last changes fastest.
Arguments:
- single_site: float32 [256, 2, 2, 1024], P('atom', 'energy'), may hold values from -2 to 2
- structure: float32 [2, 26, 2, 1024], P('energy'), may hold values from -0.4375 to 0.4375
- neighbours: int32 [256, 26], P('atom'), may hold values from 0 to 255, as said below
- species: int32 [256], P('atom'), may hold values from 0 to 1
- valence: float32 [2], replicated, may hold values from 0.5 to 3
- energy_weights: float32 [2, 2], P('energy'), may hold values from -4 to 4
- gaunt_table: float32 [49, 1024], replicated, may hold values from -1.5 to 1.5
- radial_shapes: float32 [2, 2, 2, 49, 512], P(None, 'energy'), may hold values from -6 to 6
- radial_weights: float32 [512], replicated, may hold values from 0.001 to 0.03
- madelung: float32 [256, 256], P('atom'), may hold values from -0.375 to 0.375
- old_potential: float32 [256, 49, 512], P('atom', None, 'energy'), may hold values from -6 to 6
Outputs:
- density: float32 [256, 49, 512], P('atom', None, 'energy')
- potential: float32 [256, 49, 512], P('atom', None, 'energy')
The draws below stay inside these ranges and needn't reach their ends.
Inputs may be any that keep to these rules, and one draw needn't show every extreme that they name: `neighbours`: atom a lies in lattice plane a // 16; the 16 planes close periodically. Slots 0 to 8 name distinct atoms of the plane before a's, slots 9 to 16 distinct atoms of a's own plane other than a, slots 17 to 25 distinct atoms of the plane after. Direction 26 - 1 - k is the reverse of direction k; this only says which structure constants pair up, and the neighbour lists need not be reciprocal.
All inputs are finite; a program needn't handle non-finite values.
Results may differ from the reference program's by a relative error of at most 0.0001.
Values sent between devices are 32-bit elements; how exact they have to be, the bound alone decides.
A program may use at most 64 MiB of HBM per device.

```python
import math
import jax
import jax.numpy as jnp
from jax import lax

ORDER = 32
DIRS = 26
LM = 49
RADIAL = 512
PLANE = 16
TERMS = 4
SPECIES = 2
ATOMS = 256
ENERGIES = 2


def draw_neighbours(key, part):
    plane_count = ATOMS // PLANE
    atom_ids = jnp.arange(ATOMS, dtype=jnp.int32)
    plane_index = atom_ids // PLANE
    position = atom_ids % PLANE
    slots = jnp.arange(PLANE, dtype=jnp.int32)[None, :]
    columns = []
    for offset, picked, stream in ((-1, 9, 11), (0, 8, 12), (1, 9, 13)):
        scores = jax.random.randint(jax.random.fold_in(key, stream), (ATOMS, PLANE), 0, 1 << 20, dtype=jnp.int32) * PLANE + slots
        if offset == 0:
            scores = jnp.where(slots == position[:, None], jnp.int32(1 << 30), scores)
        ranking = jnp.argsort(scores, axis=1)[:, :picked].astype(jnp.int32)
        target = ((plane_index + offset) % plane_count)[:, None] * PLANE + ranking
        columns.append(target)
    return jnp.concatenate(columns, axis=1).astype(jnp.int32)


def plant(values, own_key, smallest, largest):
    place = [jax.random.randint(jax.random.fold_in(own_key, axis), (), 0, length) for axis, length in enumerate(values.shape)]
    widest = values.shape.index(max(values.shape))
    beside = place[:widest] + [(place[widest] + 1) % values.shape[widest]] + place[widest + 1:]
    return values.at[tuple(place)].set(smallest).at[tuple(beside)].set(largest)


def shard_levels(key, shape, split, smallest, high):
    level, own = 1.0, jax.random.fold_in(key, 6)
    for dim, shards_of in split:
        heights = jnp.exp(jax.random.uniform(jax.random.fold_in(own, dim), (shards_of,), jnp.float32, smallest / len(split), high / len(split)))
        level = level * jnp.repeat(heights, shape[dim] // shards_of).reshape([-1 if axis == dim else 1 for axis in range(len(shape))])
    return level


def centred(own_key, extent, width, bound, cuts=(), kind=jnp.bfloat16):
    values = width * jax.random.normal(own_key, extent, jnp.float32)
    if cuts:
        values = values * shard_levels(own_key, extent, cuts, -0.22, 0.18)
    return jnp.clip(values, -bound, bound).astype(kind)


def setup_inputs(seed: int = 0) -> dict:
    key_list = jax.random.split(jax.random.key(seed), 12)
    return {
        "single_site": centred(key_list[0], (ATOMS, ENERGIES, 2, ORDER * ORDER), 0.125, 2.0, ((0, 16), (1, 2)), jnp.float32),
        "structure": centred(key_list[1], (ENERGIES, DIRS, 2, ORDER * ORDER), 0.03, 0.4375, ((0, 2),), jnp.float32),
        "neighbours": draw_neighbours(jax.random.fold_in(key_list[11], 71), 0),
        "species": plant(jax.random.randint(key_list[3], (ATOMS,), 0, SPECIES), jax.random.fold_in(key_list[3], 1), 0, SPECIES - 1).astype(jnp.int32),
        "valence": jnp.clip(jax.random.uniform(key_list[4], (SPECIES,), jnp.float32, 0.5, 3.0), 0.5, 3.0),
        "energy_weights": centred(key_list[5], (ENERGIES, 2), 1.0, 4.0, ((0, 2),), jnp.float32),
        "gaunt_table": centred(key_list[6], (LM, ORDER * ORDER), 16 ** -0.5, 1.5, (), jnp.float32),
        "radial_shapes": centred(key_list[7], (SPECIES, ENERGIES, 2, LM, RADIAL), 1.0, 6.0, ((1, 2),), jnp.float32),
        "radial_weights": jnp.clip(jnp.exp(jax.random.uniform(key_list[8], (RADIAL,), jnp.float32, math.log(0.001), math.log(0.03))), 0.001, 0.03),
        "madelung": centred(key_list[9], (ATOMS, ATOMS), ATOMS ** -0.5, 0.375, ((0, 16),), jnp.float32),
        "old_potential": centred(key_list[10], (ATOMS, LM, RADIAL), 1.0, 6.0, ((0, 16), (2, 2)), jnp.float32),
    }


mixing = 0.3
highest = lax.Precision.HIGHEST


def matmul_high(former, latter):
    return jnp.matmul(former, latter, precision=highest)


def complex_product(former, latter):
    former_real = former[..., 0, :, :]
    former_imag = former[..., 1, :, :]
    latter_real = latter[..., 0, :, :]
    latter_imag = latter[..., 1, :, :]
    real_part = matmul_high(former_real, latter_real) - matmul_high(former_imag, latter_imag)
    imag_part = matmul_high(former_real, latter_imag) + matmul_high(former_imag, latter_real)
    return jnp.stack([real_part, imag_part], axis=-3)


def reference(single_site, structure, neighbours, species, valence, energy_weights, gaunt_table, radial_shapes, radial_weights, madelung, old_potential):
    site_matrices = single_site.reshape(ATOMS, ENERGIES, 2, ORDER, ORDER)
    couplings = structure.reshape(ENERGIES, DIRS, 2, ORDER, ORDER)

    def add_direction(accumulated, direction):
        forward = lax.dynamic_index_in_dim(couplings, direction, 1, keepdims=False)
        backward = lax.dynamic_index_in_dim(couplings, DIRS - 1 - direction, 1, keepdims=False)
        column = lax.dynamic_index_in_dim(neighbours, direction, 1, keepdims=False)
        gathered = jnp.take(site_matrices, column, axis=0)
        return accumulated + complex_product(complex_product(forward, gathered), backward), None

    coupled, _ = lax.scan(add_direction, jnp.zeros_like(site_matrices), jnp.arange(DIRS, dtype=jnp.int32))
    propagator = complex_product(site_matrices, coupled)
    series_term = site_matrices
    path_operator = site_matrices
    for power in range(TERMS - 1):
        series_term = complex_product(propagator, series_term)
        path_operator = path_operator + series_term
    flat = path_operator.reshape(ATOMS, ENERGIES, 2, ORDER * ORDER)
    projected = jnp.einsum('aezq,lq->aezl', flat, gaunt_table, precision=highest)
    weight_real = energy_weights[:, 0][None, :, None]
    weight_imag = energy_weights[:, 1][None, :, None]
    scaled_real = weight_real * projected[:, :, 0] - weight_imag * projected[:, :, 1]
    scaled_imag = weight_real * projected[:, :, 1] + weight_imag * projected[:, :, 0]
    kinds = jnp.arange(SPECIES, dtype=jnp.int32)
    one_hot = jnp.where(species[:, None] == kinds[None, :], jnp.float32(1.0), jnp.float32(0.0))
    sorted_real = one_hot[:, :, None, None] * scaled_real[:, None]
    sorted_imag = one_hot[:, :, None, None] * scaled_imag[:, None]
    density = jnp.einsum('asel,selr->alr', sorted_real, radial_shapes[:, :, 1], precision=highest)
    density = density + jnp.einsum('asel,selr->alr', sorted_imag, radial_shapes[:, :, 0], precision=highest)
    valence_of = jnp.sum(one_hot * valence[None, :], axis=1)
    charges = jnp.dot(density[:, 0, :], radial_weights, precision=highest) - valence_of
    madelung_shift = jnp.dot(madelung, charges, precision=highest)
    channel = jnp.arange(LM, dtype=jnp.int32)[None, :, None]
    added = jnp.where(channel == 0, madelung_shift[:, None, None], jnp.float32(0.0))
    potential = (1.0 - mixing) * old_potential + mixing * (density + added)
    return density, potential
```

```python
import functools

import jax
import jax.numpy as jnp
from jax import lax
from jax.experimental import pallas as pl
from jax.experimental.pallas import tpu as pltpu
from jax.sharding import PartitionSpec as P

PLANE = 16
LANES = 128
ROWS = 8
CHUNKS = 4

mixing = 0.3
f32 = jnp.float32
bf16 = jnp.bfloat16


def split(x):
    high = x.astype(bf16)
    return high, (x - high.astype(f32)).astype(bf16)


def dot(a, b):
    return jnp.dot(a, b, preferred_element_type=f32)


def lane_masks(rows):
    lane = lax.broadcasted_iota(jnp.int32, (rows, LANES), 1)
    return lane < 64, (lane & 32) == 0


def times_i(x, real_lane):
    return jnp.where(real_lane, -pltpu.roll(x, 96, 1), pltpu.roll(x, 32, 1))


def swap_blocks(parts):
    low, even = lane_masks(parts[0].shape[0])
    near = []
    for a, b in ((parts[0], parts[1]), (parts[2], parts[3])):
        near.append((jnp.where(even, a, pltpu.roll(b, 32, 1)), jnp.where(even, pltpu.roll(a, 96, 1), b)))
    out = [None] * 4
    for j in range(2):
        c, d = near[0][j], near[1][j]
        out[j] = jnp.where(low, c, pltpu.roll(d, 64, 1))
        out[j + 2] = jnp.where(low, pltpu.roll(c, 64, 1), d)
    return out


def to_tile(raw, out_ref):
    rows = swap_blocks([raw(m) for m in range(4)])
    for ii in range(4):
        out_ref[pl.ds(ii, ROWS, stride=4), :] = rows[ii]


def packed(x):
    high, low = split(x)
    half = LANES // 2
    even = jnp.concatenate([high[:, :half], low[:, :half]], axis=1)
    odd = jnp.concatenate([high[:, half:], low[:, half:]], axis=1)
    return even, odd


def block_diagonal(v, low_lane, real_lane):
    turned = times_i(v, real_lane)
    zero = jnp.zeros_like(v)
    return jnp.concatenate(
        [
            jnp.where(low_lane, v, zero),
            jnp.where(low_lane, turned, zero),
            jnp.where(low_lane, zero, v),
            jnp.where(low_lane, zero, turned),
        ],
        axis=0,
    )


def weights_of(v, low_lane, real_lane):
    high, low = split(block_diagonal(v, low_lane, real_lane))
    return jnp.concatenate([high, low], axis=1)


def pair_product(u, weights):
    rows = u.shape[0]
    high, low = split(u)
    o = dot(jnp.concatenate([high, low], axis=0), weights)
    return o[:rows, :LANES] + o[rows:, :LANES] + o[:rows, LANES:]


def ends_of(dirs):
    return ((0, 9), (9, 17), (17, dirs))


def plane_products(tiles, gx_ref, l_ref, start, stop, order):
    count = stop - start
    lhs = gx_ref[start:stop, :order, :].reshape(count * order, LANES)
    lhs = jnp.concatenate([lhs, lhs], axis=1)
    _, real_lane = lane_masks(order)
    for quad in range(PLANE // 4):
        columns = []
        for pair in (2 * quad, 2 * quad + 1):
            v = tiles[pair]
            high, low = split(jnp.concatenate([v, times_i(v, real_lane)], axis=0))
            columns.append(jnp.concatenate([high, high, low, low], axis=0))
        r = dot(lhs, jnp.concatenate(columns, axis=1))
        for h in range(2):
            even, odd = packed(r[:, h * LANES : (h + 1) * LANES])
            n = 4 * quad + 2 * h
            l_ref[start:stop, n] = even.reshape(count, order, LANES)
            l_ref[start:stop, n + 1] = odd.reshape(count, order, LANES)


def plane_sum(nbr_ref, gx_ref, l_ref, start, stop, dirs):
    lhs, rhs = [], []
    for a in range(PLANE):
        lhs.append(jnp.concatenate([l_ref[k, nbr_ref[a, k] & (PLANE - 1)] for k in range(start, stop)], axis=1))
    for k in range(start, stop):
        g = gx_ref[dirs - 1 - k]
        rhs += [g, g]
    return dot(jnp.concatenate(lhs, axis=0), jnp.concatenate(rhs, axis=0))


def project(tiles, total, wd_ref, table_ref, v_ref, order):
    low_lane, real_lane = lane_masks(order)
    pairs = range(PLANE // 2)
    cs = []
    for pair in pairs:
        even = total[2 * pair * order : (2 * pair + 1) * order]
        odd = total[(2 * pair + 1) * order : (2 * pair + 2) * order]
        cs.append(jnp.where(low_lane, even, odd) + pltpu.roll(jnp.where(low_lane, odd, even), 64, 1))
    qs = [pair_product(cs[pair], wd_ref[pair]) for pair in pairs]
    ws = [weights_of(q, low_lane, real_lane) for q in qs]
    ts = [tiles[pair] for pair in pairs]
    ys = [pair_product(jnp.concatenate([ts[pair], qs[pair]], axis=0), ws[pair]) for pair in pairs]
    vs = [ts[pair] + ys[pair][:order] for pair in pairs]
    ws = [weights_of(y[order:], low_lane, real_lane) for y in ys]
    for pair in pairs:
        v_ref[pl.ds(pair * order, order), :] = vs[pair] + pair_product(vs[pair], ws[pair])
    columns = []
    for block in range(order // 4):
        us = [v_ref[pl.ds(4 * block + ii, PLANE // 2, stride=order), :] for ii in range(4)]
        columns.append(jnp.concatenate(swap_blocks(us), axis=0))
    z = jnp.concatenate(columns, axis=1)
    zh, zl = split(z)
    nt = (((1,), (1,)), ((), ()))
    d = lax.dot_general(jnp.concatenate([zh, zl], axis=0), table_ref[...], nt, preferred_element_type=f32)
    rows = 2 * PLANE
    return d[:rows] + d[rows:] + pltpu.roll(d[:rows], 64, 1)


def store_scaled(projected, wr, wi, coef_ref):
    pairs = PLANE // 2
    channels = coef_ref.shape[2]
    for a2 in range(2):
        re = projected[a2 * 2 * pairs : a2 * 2 * pairs + pairs, :channels]
        im = projected[a2 * 2 * pairs + pairs : (a2 + 1) * 2 * pairs, :channels]
        coef_ref[0, pl.ds(a2, pairs, stride=2), :] = wr * re - wi * im
        coef_ref[1, pl.ds(a2, pairs, stride=2), :] = wr * im + wi * re


def density_of(kind, coef_ref, pieces_ref, old_ref, density_ref, potential_ref):
    energies, kinds = pieces_ref.shape[:2]
    channels, atoms, width = density_ref.shape
    kind = jnp.broadcast_to(kind, (atoms, width))
    for l in range(channels):
        total = None
        for e in range(energies):
            for z in range(2):
                row = jnp.broadcast_to(pieces_ref[e, 0, l, 1 - z : 2 - z, :], (atoms, width))
                for s in range(1, kinds):
                    row = jnp.where(kind == s, pieces_ref[e, s, l, 1 - z : 2 - z, :], row)
                term = coef_ref[e, z, :, l : l + 1] * row
                total = term if total is None else total + term
        density_ref[l] = total
        if l > 0:
            potential_ref[l] = (1.0 - mixing) * old_ref[l] + mixing * total


def far_rounds(ring):
    rounds = 0
    while 2**rounds < ring // 2:
        rounds += 1
    return rounds


def core(order, dirs, ring, energies,
         nbr_hbm, w_hbm, valence_hbm, own_hbm, g_hbm, gaunt_hbm, shapes_hbm, weights_hbm, species_hbm,
         madelung_hbm, previous_hbm, density_ref, potential_ref,
         nbr_ref, w_ref, valence_ref, own_ref, g_ref, gaunt_ref, lowest_ref, weights_ref, species_ref,
         madelung_ref, old_ref, pieces_ref, coef_ref, mine_ref, q_ref, halo_ref,
         gtile_ref, tile_ref, gx_ref, l_ref, wd_ref, table_ref, v_ref,
         load_sem, keep_sem, halo_send, halo_recv, piece_send, piece_recv, coef_send, coef_recv,
         q_send, q_recv, far_sem):
    atom, energy = lax.axis_index("atom"), lax.axis_index("energy")
    devices = ring * energies
    me = atom * energies + energy
    kinds, width = shapes_hbm.shape[0], pieces_ref.shape[4]
    channels = gaunt_ref.shape[0]
    ends = ends_of(dirs)

    def ahead(step):
        return {"atom": lax.rem(atom + step + ring, ring), "energy": energy}

    def peer(step):
        return {"atom": atom, "energy": lax.rem(energy + step, energies)}

    barrier = pltpu.get_barrier_semaphore()
    near = [ahead(1), ahead(-1)] + [peer(step) for step in range(1, energies)]
    for place in near:
        pl.semaphore_signal(barrier, inc=1, device_id=place, device_id_type=MESH)

    sources = [(own_hbm, own_ref), (g_hbm, g_ref), (nbr_hbm, nbr_ref), (gaunt_hbm, gaunt_ref),
               (shapes_hbm.at[:, 0], lowest_ref), (weights_hbm, weights_ref), (species_hbm, species_ref),
               (w_hbm, w_ref), (valence_hbm, valence_ref), (madelung_hbm, madelung_ref), (previous_hbm, old_ref)]
    loads = []
    for i, (src, dst) in enumerate(sources):
        loads.append(pltpu.make_async_copy(src, dst, load_sem.at[i]))
        loads[-1].start()

    loads[0].wait()
    pl.semaphore_wait(barrier, len(near))
    rounds = far_rounds(ring)

    def tell(index):
        places = [ahead(2**index), ahead(-(2**index))] if index < rounds else near[2:]
        for place in places:
            pl.semaphore_signal(far_sem.at[index], inc=1, device_id=place, device_id_type=MESH)

    def hear(index):
        pl.semaphore_wait(far_sem.at[index], 2 if index < rounds else energies - 1)

    tell(0)
    halos = []
    for side, step in ((0, 1), (1, -1)):
        copy = pltpu.make_async_remote_copy(
            src_ref=own_ref, dst_ref=halo_ref.at[side], send_sem=halo_send.at[side],
            recv_sem=halo_recv.at[side], device_id=ahead(step), device_id_type=MESH,
        )
        copy.start()
        halos.append(copy)

    def slice_of(e):
        return shapes_hbm.at[:, :, :, pl.ds(pl.multiple_of(e * width, LANES), width)]

    pieces = []
    for step in range(1, energies):
        copy = pltpu.make_async_remote_copy(
            src_ref=slice_of(lax.rem(energy + step, energies)), dst_ref=pieces_ref.at[energy],
            send_sem=piece_send.at[step], recv_sem=piece_recv.at[step], device_id=peer(step), device_id_type=MESH,
        )
        copy.start()
        pieces.append(copy)
    keep = pltpu.make_async_copy(slice_of(energy), pieces_ref.at[energy], keep_sem)
    keep.start()

    loads[1].wait()
    low_lane, real_lane = lane_masks(order)
    for t in range(dirs // 2):
        to_tile(lambda m: g_ref[2 * t + m // 2, pl.ds(m % 2, ROWS, stride=2), :], gtile_ref.at[t])
        g = gtile_ref[t]
        even, odd = packed(jnp.concatenate([g, times_i(g, real_lane)], axis=0))
        gx_ref[2 * t] = even
        gx_ref[2 * t + 1] = odd

    def products(index, ref):
        for pair in range(PLANE // 2):
            to_tile(lambda m: ref[2 * pair + m // 2, pl.ds(m % 2, ROWS, stride=2), :], tile_ref.at[index, pair])
        plane_products(tile_ref.at[index], gx_ref, l_ref, *ends[index], order)

    products(1, own_ref)
    loads[2].wait()
    own_sum = plane_sum(nbr_ref, gx_ref, l_ref, *ends[1], dirs)

    for pair in range(PLANE // 2):
        wd_ref[pair] = weights_of(tile_ref[1, pair], low_lane, real_lane)
    loads[3].wait()
    high, low = split(gaunt_ref[...])
    table_ref[...] = jnp.zeros(table_ref.shape, bf16)
    table_ref[pl.ds(0, channels), :] = high
    table_ref[pl.ds(64, channels), :] = low

    for load in loads[4:10]:
        load.wait()
    row = lax.broadcasted_iota(jnp.int32, (PLANE, PLANE), 0)
    lane = lax.broadcasted_iota(jnp.int32, (PLANE, PLANE), 1)
    kinds_row = jnp.broadcast_to(species_ref[...].astype(f32), (PLANE, PLANE))
    kind = jnp.sum(jnp.where(row == lane, kinds_row, jnp.zeros((PLANE, PLANE), f32)), axis=1, keepdims=True)
    sums = [None, None]
    base = jnp.zeros(kind.shape, f32)
    for s in range(kinds):
        total = jnp.sum(lowest_ref[s] * weights_ref[...], axis=1, keepdims=True)
        for z in range(2):
            value = jnp.broadcast_to(total[1 - z : 2 - z], kind.shape)
            sums[z] = value if s == 0 else jnp.where(kind == s, value, sums[z])
        base = jnp.where(kind == s, valence_ref[s], base)
    base = jnp.where(energy == 0, base, jnp.zeros_like(base))

    total = own_sum
    hear(0)
    tell(1)
    halos[0].wait_recv()
    products(0, halo_ref.at[0])
    total = total + plane_sum(nbr_ref, gx_ref, l_ref, *ends[0], dirs)
    hear(1)
    tell(2)
    halos[1].wait_recv()
    products(2, halo_ref.at[1])
    total = total + plane_sum(nbr_ref, gx_ref, l_ref, *ends[2], dirs)
    for index in range(2, rounds):
        hear(index)
        tell(index + 1)

    projected = project(tile_ref.at[1], total, wd_ref, table_ref, v_ref, order)
    store_scaled(projected, w_ref[0, 0], w_ref[0, 1], mine_ref)

    q = mine_ref[0, :, 0:1] * sums[0] + mine_ref[1, :, 0:1] * sums[1] - base
    row = lax.broadcasted_iota(jnp.int32, (PLANE, LANES), 0)
    lane = lax.broadcasted_iota(jnp.int32, (PLANE, LANES), 1)
    spot = lane == row + PLANE * lax.rem(atom, LANES // PLANE)
    q_ref[me] = jnp.sum(jnp.where(spot, q, jnp.zeros((PLANE, LANES), f32)), axis=0, keepdims=True)
    hear(rounds)

    def spread(step, carry):
        other = lax.rem(me + step, devices)
        pltpu.make_async_remote_copy(
            src_ref=q_ref.at[me], dst_ref=q_ref.at[me], send_sem=q_send, recv_sem=q_recv,
            device_id={"atom": other // energies, "energy": lax.rem(other, energies)}, device_id_type=MESH,
        ).start()
        return carry

    lax.fori_loop(1, devices, spread, 0)
    coefs = []
    for step in range(1, energies):
        copy = pltpu.make_async_remote_copy(
            src_ref=mine_ref, dst_ref=coef_ref.at[energy], send_sem=coef_send.at[step],
            recv_sem=coef_recv.at[step], device_id=peer(step), device_id_type=MESH,
        )
        copy.start()
        coefs.append(copy)
    coef_ref[energy] = mine_ref[...]

    keep.wait()
    loads[10].wait()
    for copy in pieces + coefs:
        copy.wait()
    density_of(kind, coef_ref, pieces_ref, old_ref, density_ref, potential_ref)
    for copy in halos:
        copy.wait_send()
    rest = q_ref.at[pl.ds(0, devices - 1)]
    pltpu.make_async_copy(rest, rest, q_send).wait()
    pltpu.make_async_copy(rest, rest, q_recv).wait()
    group = LANES // PLANE * energies
    shift = jnp.zeros((PLANE, 1), f32)
    for g in range(ring * PLANE // LANES):
        charges = jnp.sum(q_ref[pl.ds(g * group, group), 0, :], axis=0, keepdims=True)
        shift = shift + jnp.sum(madelung_ref[:, pl.ds(g * LANES, LANES)] * charges, axis=1, keepdims=True)
    potential_ref[0] = (1.0 - mixing) * old_ref[0] + mixing * (density_ref[0] + shift)


def core_scratch(order, dirs, ring, energies, channels, kinds, width):
    dma = pltpu.SemaphoreType.DMA
    return [
        pltpu.SMEM((PLANE, dirs), jnp.int32),
        pltpu.SMEM((1, 2), f32),
        pltpu.SMEM((kinds,), f32),
        pltpu.VMEM((PLANE, 2 * ROWS, LANES), f32),
        pltpu.VMEM((dirs, 2 * ROWS, LANES), f32),
        pltpu.VMEM((channels, order * order), f32),
        pltpu.VMEM((kinds, 2, width * energies), f32),
        pltpu.VMEM((1, width * energies), f32),
        pltpu.VMEM((1, PLANE), jnp.int32),
        pltpu.VMEM((PLANE, ring * PLANE), f32),
        pltpu.VMEM((channels, PLANE, width), f32),
        pltpu.VMEM((energies, kinds, channels, 2, width), f32),
        pltpu.VMEM((energies, 2, PLANE, channels), f32),
        pltpu.VMEM((2, PLANE, channels), f32),
        pltpu.VMEM((ring * energies, 1, LANES), f32),
        pltpu.VMEM((2, PLANE, 2 * ROWS, LANES), f32),
        pltpu.VMEM((dirs // 2, order, LANES), f32),
        pltpu.VMEM((3, PLANE // 2, order, LANES), f32),
        pltpu.VMEM((dirs, 2 * order, LANES), bf16),
        pltpu.VMEM((dirs, PLANE, order, LANES), bf16),
        pltpu.VMEM((PLANE // 2, LANES, 2 * LANES), bf16),
        pltpu.VMEM((LANES, order * order), bf16),
        pltpu.VMEM((PLANE // 2 * order, LANES), f32),
        dma((11,)), dma, dma((2,)), dma((2,)), dma((energies,)), dma((energies,)), dma((energies,)),
        dma((energies,)), dma, dma, pltpu.SemaphoreType.REGULAR((far_rounds(ring) + 1,)),
    ]


def emit(density_ref, potential_ref, density_out, potential_out, sems):
    channels = density_ref.shape[0]
    edges = [channels * i // CHUNKS for i in range(CHUNKS + 1)]
    copies = []
    for i in range(CHUNKS):
        part = pl.ds(edges[i], edges[i + 1] - edges[i])
        for j, (src, dst) in enumerate(((density_ref, density_out), (potential_ref, potential_out))):
            copies.append(pltpu.make_async_copy(src.at[part], dst.at[part], sems.at[2 * i + j]))
            copies[-1].start()
    for copy in copies:
        copy.wait()


VMEM = pl.BlockSpec(memory_space=pltpu.VMEM)
ANY = pl.BlockSpec(memory_space=pl.ANY)
HBM = pl.BlockSpec(memory_space=pltpu.HBM)
MESH = pl.DeviceIdType.MESH


def shards(single_site, structure, neighbours, species, valence, energy_weights, gaunt_table,
           radial_shapes, radial_weights, madelung, old_potential):
    atom_rows, energy_rows = single_site.shape[:2]
    dirs = structure.shape[1]
    order = int(round(single_site.shape[3] ** 0.5))
    channels, width = old_potential.shape[1], old_potential.shape[2]
    kinds = radial_shapes.shape[0]
    energies = lax.axis_size("energy")
    assert atom_rows == PLANE and energy_rows == 1 and order == 32 and channels <= 64

    def parts(x):
        x = x.reshape(-1, 2, order * order // LANES, LANES)
        return jnp.transpose(x, (0, 2, 1, 3)).reshape(-1, 2 * ROWS, LANES)

    shapes = jnp.transpose(radial_shapes[:, 0], (0, 2, 1, 3))
    ring = lax.axis_size("atom")
    whole = [jax.ShapeDtypeStruct((channels, atom_rows, width), f32)] * 2
    operands = (neighbours, energy_weights, valence, parts(single_site), parts(structure), gaunt_table, shapes,
                radial_weights[None, :], species[None, :], madelung, jnp.transpose(old_potential, (1, 0, 2)))
    density, potential = pl.pallas_call(
        functools.partial(core, order, dirs, ring, energies),
        out_shape=whole,
        in_specs=[HBM] * 11,
        out_specs=[VMEM] * 2,
        scratch_shapes=core_scratch(order, dirs, ring, energies, channels, kinds, width),
        compiler_params=pltpu.CompilerParams(
            collective_id=0, has_side_effects=True, vmem_limit_bytes=32 * 1024 * 1024
        ),
        name="scatter",
    )(*(pltpu.with_memory_space_constraint(x, pltpu.HBM) for x in operands))
    density, potential = pl.pallas_call(
        emit,
        out_shape=whole,
        in_specs=[ANY] * 2,
        out_specs=[ANY] * 2,
        scratch_shapes=[pltpu.SemaphoreType.DMA((2 * CHUNKS,))],
        compiler_params=pltpu.CompilerParams(vmem_limit_bytes=1024 * 1024),
        name="emit",
    )(density, potential)

    back = lambda x: jnp.transpose(x, (1, 0, 2))
    return back(density), back(potential)


def solution(mesh):
    in_specs = (
        P("atom", "energy", None, None),
        P("energy", None, None, None),
        P("atom", None),
        P("atom"),
        P(),
        P("energy", None),
        P(),
        P(None, "energy", None, None, None),
        P(),
        P("atom", None),
        P("atom", None, "energy"),
    )
    out_specs = (P("atom", None, "energy"), P("atom", None, "energy"))
    return jax.shard_map(shards, mesh=mesh, in_specs=in_specs, out_specs=out_specs, check_vma=False)
```

```python
import functools

import jax
import jax.numpy as jnp
from jax import lax
from jax.experimental import pallas as pl
from jax.experimental.pallas import tpu as pltpu
from jax.sharding import PartitionSpec as P

PLANE = 16
LANES = 128
ROWS = 8
CHUNKS = 4
PARTS = 1

mixing = 0.3
f32 = jnp.float32
bf16 = jnp.bfloat16


def split(x):
    high = x.astype(bf16)
    return high, (x - high.astype(f32)).astype(bf16)


def dot(a, b):
    return jnp.dot(a, b, preferred_element_type=f32)


def lane_masks(rows):
    lane = lax.broadcasted_iota(jnp.int32, (rows, LANES), 1)
    return lane < 64, (lane & 32) == 0


def times_i(x, real_lane):
    return jnp.where(real_lane, -pltpu.roll(x, 96, 1), pltpu.roll(x, 32, 1))


def swap_blocks(parts):
    low, even = lane_masks(parts[0].shape[0])
    near = []
    for a, b in ((parts[0], parts[1]), (parts[2], parts[3])):
        near.append((jnp.where(even, a, pltpu.roll(b, 32, 1)), jnp.where(even, pltpu.roll(a, 96, 1), b)))
    out = [None] * 4
    for j in range(2):
        c, d = near[0][j], near[1][j]
        out[j] = jnp.where(low, c, pltpu.roll(d, 64, 1))
        out[j + 2] = jnp.where(low, pltpu.roll(c, 64, 1), d)
    return out


def to_tile(raw, out_ref):
    rows = swap_blocks([raw(m) for m in range(4)])
    for ii in range(4):
        out_ref[pl.ds(ii, ROWS, stride=4), :] = rows[ii]


def packed(x):
    high, low = split(x)
    half = LANES // 2
    even = jnp.concatenate([high[:, :half], low[:, :half]], axis=1)
    odd = jnp.concatenate([high[:, half:], low[:, half:]], axis=1)
    return even, odd


def block_diagonal(v, low_lane, real_lane):
    turned = times_i(v, real_lane)
    zero = jnp.zeros_like(v)
    return jnp.concatenate(
        [
            jnp.where(low_lane, v, zero),
            jnp.where(low_lane, turned, zero),
            jnp.where(low_lane, zero, v),
            jnp.where(low_lane, zero, turned),
        ],
        axis=0,
    )


def weights_of(v, low_lane, real_lane):
    high, low = split(block_diagonal(v, low_lane, real_lane))
    return jnp.concatenate([high, low], axis=1)


def pair_product(u, weights):
    rows = u.shape[0]
    high, low = split(u)
    o = dot(jnp.concatenate([high, low], axis=0), weights)
    return o[:rows, :LANES] + o[rows:, :LANES] + o[:rows, LANES:]


def ends_of(dirs):
    return ((0, 9), (9, 17), (17, dirs))


def plane_products(tiles, gx_ref, l_ref, start, stop, order):
    count = stop - start
    lhs = gx_ref[start:stop, :order, :].reshape(count * order, LANES)
    lhs = jnp.concatenate([lhs, lhs], axis=1)
    _, real_lane = lane_masks(order)
    for quad in range(PLANE // 4):
        columns = []
        for pair in (2 * quad, 2 * quad + 1):
            v = tiles[pair]
            high, low = split(jnp.concatenate([v, times_i(v, real_lane)], axis=0))
            columns.append(jnp.concatenate([high, high, low, low], axis=0))
        r = dot(lhs, jnp.concatenate(columns, axis=1))
        for h in range(2):
            even, odd = packed(r[:, h * LANES : (h + 1) * LANES])
            n = 4 * quad + 2 * h
            l_ref[:count, n] = even.reshape(count, order, LANES)
            l_ref[:count, n + 1] = odd.reshape(count, order, LANES)


def plane_sum(nbr_ref, gx_ref, l_ref, start, stop, dirs, atoms):
    lhs, rhs = [], []
    for a in atoms:
        lhs.append(jnp.concatenate([l_ref[k - start, nbr_ref[a, k] & (PLANE - 1)] for k in range(start, stop)], axis=1))
    for k in range(start, stop):
        g = gx_ref[dirs - 1 - k]
        rhs += [g, g]
    return dot(jnp.concatenate(lhs, axis=0), jnp.concatenate(rhs, axis=0))


def series(tiles, total, wd_ref, v_ref, atoms, order):
    low_lane, real_lane = lane_masks(order)
    pairs = range(atoms[0] // 2, atoms[-1] // 2 + 1)
    cs = {}
    for i, pair in enumerate(pairs):
        even = total[2 * i * order : (2 * i + 1) * order]
        odd = total[(2 * i + 1) * order : (2 * i + 2) * order]
        cs[pair] = jnp.where(low_lane, even, odd) + pltpu.roll(jnp.where(low_lane, odd, even), 64, 1)
    ts = {pair: tiles[pair] for pair in pairs}
    qs = {pair: pair_product(cs[pair], wd_ref[pair]) for pair in pairs}
    ws = {pair: weights_of(qs[pair], low_lane, real_lane) for pair in pairs}
    ys = {pair: pair_product(jnp.concatenate([ts[pair], qs[pair]], axis=0), ws[pair]) for pair in pairs}
    vs = {pair: ts[pair] + ys[pair][:order] for pair in pairs}
    ws = {pair: weights_of(ys[pair][order:], low_lane, real_lane) for pair in pairs}
    for pair in pairs:
        v_ref[pl.ds(pair * order, order), :] = vs[pair] + pair_product(vs[pair], ws[pair])


def project(table_ref, v_ref, order):
    columns = []
    for block in range(order // 4):
        us = [v_ref[pl.ds(4 * block + ii, PLANE // 2, stride=order), :] for ii in range(4)]
        columns.append(jnp.concatenate(swap_blocks(us), axis=0))
    z = jnp.concatenate(columns, axis=1)
    zh, zl = split(z)
    nt = (((1,), (1,)), ((), ()))
    d = lax.dot_general(jnp.concatenate([zh, zl], axis=0), table_ref[...], nt, preferred_element_type=f32)
    rows = 2 * PLANE
    return d[:rows] + d[rows:] + pltpu.roll(d[:rows], 64, 1)


def store_scaled(projected, wr, wi, coef_ref):
    pairs = PLANE // 2
    channels = coef_ref.shape[2]
    for a2 in range(2):
        re = projected[a2 * 2 * pairs : a2 * 2 * pairs + pairs, :channels]
        im = projected[a2 * 2 * pairs + pairs : (a2 + 1) * 2 * pairs, :channels]
        coef_ref[0, pl.ds(a2, pairs, stride=2), :] = wr * re - wi * im
        coef_ref[1, pl.ds(a2, pairs, stride=2), :] = wr * im + wi * re


def density_of(kind, coef_ref, pieces_ref, old_ref, density_ref, potential_ref):
    energies, kinds = pieces_ref.shape[:2]
    channels, atoms, width = density_ref.shape
    kind = jnp.broadcast_to(kind, (atoms, width))
    for l in range(channels):
        total = None
        for e in range(energies):
            for z in range(2):
                row = jnp.broadcast_to(pieces_ref[e, 0, l, 1 - z : 2 - z, :], (atoms, width))
                for s in range(1, kinds):
                    row = jnp.where(kind == s, pieces_ref[e, s, l, 1 - z : 2 - z, :], row)
                term = coef_ref[e, z, :, l : l + 1] * row
                total = term if total is None else total + term
        density_ref[l] = total
        if l > 0:
            potential_ref[l] = (1.0 - mixing) * old_ref[l] + mixing * total


def far_rounds(ring):
    rounds = 0
    while 2**rounds < ring // 2:
        rounds += 1
    return rounds


def core(order, dirs, ring, energies,
         nbr_hbm, w_hbm, valence_hbm, own_hbm, g_hbm, gaunt_hbm, shapes_hbm, weights_hbm, species_hbm,
         madelung_hbm, previous_hbm, density_ref, potential_ref,
         nbr_ref, w_ref, valence_ref, own_ref, g_ref, gaunt_ref, lowest_ref, weights_ref, species_ref,
         madelung_ref, old_ref, pieces_ref, coef_ref, mine_ref, q_ref, halo_ref,
         gtile_ref, tile_ref, gx_ref, l0_ref, l1_ref, l2_ref, c_ref, wd_ref, table_ref, v_ref,
         load_sem, keep_sem, halo_send, halo_recv, piece_send, piece_recv, coef_send, coef_recv,
         q_send, q_recv, far_sem):
    atom, energy = lax.axis_index("atom"), lax.axis_index("energy")
    devices = ring * energies
    me = atom * energies + energy
    kinds, width = shapes_hbm.shape[0], pieces_ref.shape[4]
    channels = gaunt_ref.shape[0]
    ends = ends_of(dirs)
    l_refs = (l0_ref, l1_ref, l2_ref)

    def ahead(step):
        return {"atom": lax.rem(atom + step + ring, ring), "energy": energy}

    def peer(step):
        return {"atom": atom, "energy": lax.rem(energy + step, energies)}

    barrier = pltpu.get_barrier_semaphore()
    near = [ahead(1), ahead(-1)] + [peer(step) for step in range(1, energies)]
    for place in near:
        pl.semaphore_signal(barrier, inc=1, device_id=place, device_id_type=MESH)

    sources = [(own_hbm, own_ref), (g_hbm, g_ref), (nbr_hbm, nbr_ref), (gaunt_hbm, gaunt_ref),
               (shapes_hbm.at[:, 0], lowest_ref), (weights_hbm, weights_ref), (species_hbm, species_ref),
               (w_hbm, w_ref), (valence_hbm, valence_ref), (madelung_hbm, madelung_ref), (previous_hbm, old_ref)]
    loads = []
    for i, (src, dst) in enumerate(sources):
        loads.append(pltpu.make_async_copy(src, dst, load_sem.at[i]))
        loads[-1].start()

    loads[0].wait()
    pl.semaphore_wait(barrier, len(near))
    rounds = far_rounds(ring)

    def tell(index):
        places = [ahead(2**index), ahead(-(2**index))] if index < rounds else near[2:]
        for place in places:
            pl.semaphore_signal(far_sem.at[index], inc=1, device_id=place, device_id_type=MESH)

    def hear(index):
        pl.semaphore_wait(far_sem.at[index], 2 if index < rounds else energies - 1)

    tell(0)
    halos = []
    for side, step in ((0, 1), (1, -1)):
        copy = pltpu.make_async_remote_copy(
            src_ref=own_ref, dst_ref=halo_ref.at[side], send_sem=halo_send.at[side],
            recv_sem=halo_recv.at[side], device_id=ahead(step), device_id_type=MESH,
        )
        copy.start()
        halos.append(copy)

    def slice_of(e):
        return shapes_hbm.at[:, :, :, pl.ds(pl.multiple_of(e * width, LANES), width)]

    pieces = []
    for step in range(1, energies):
        copy = pltpu.make_async_remote_copy(
            src_ref=slice_of(lax.rem(energy + step, energies)), dst_ref=pieces_ref.at[energy],
            send_sem=piece_send.at[step], recv_sem=piece_recv.at[step], device_id=peer(step), device_id_type=MESH,
        )
        copy.start()
        pieces.append(copy)
    keep = pltpu.make_async_copy(slice_of(energy), pieces_ref.at[energy], keep_sem)
    keep.start()

    loads[1].wait()
    low_lane, real_lane = lane_masks(order)
    for t in range(dirs // 2):
        to_tile(lambda m: g_ref[2 * t + m // 2, pl.ds(m % 2, ROWS, stride=2), :], gtile_ref.at[t])
        g = gtile_ref[t]
        even, odd = packed(jnp.concatenate([g, times_i(g, real_lane)], axis=0))
        gx_ref[2 * t] = even
        gx_ref[2 * t + 1] = odd

    def products(index, ref):
        for pair in range(PLANE // 2):
            to_tile(lambda m: ref[2 * pair + m // 2, pl.ds(m % 2, ROWS, stride=2), :], tile_ref.at[index, pair])
        plane_products(tile_ref.at[index], gx_ref, l_refs[index], *ends[index], order)

    products(1, own_ref)
    loads[2].wait()
    c_ref[...] = plane_sum(nbr_ref, gx_ref, l_refs[1], *ends[1], dirs, range(PLANE))

    for pair in range(PLANE // 2):
        wd_ref[pair] = weights_of(tile_ref[1, pair], low_lane, real_lane)
    loads[3].wait()
    high, low = split(gaunt_ref[...])
    table_ref[...] = jnp.zeros(table_ref.shape, bf16)
    table_ref[pl.ds(0, channels), :] = high
    table_ref[pl.ds(64, channels), :] = low

    for load in loads[4:10]:
        load.wait()
    row = lax.broadcasted_iota(jnp.int32, (PLANE, PLANE), 0)
    lane = lax.broadcasted_iota(jnp.int32, (PLANE, PLANE), 1)
    kinds_row = jnp.broadcast_to(species_ref[...].astype(f32), (PLANE, PLANE))
    kind = jnp.sum(jnp.where(row == lane, kinds_row, jnp.zeros((PLANE, PLANE), f32)), axis=1, keepdims=True)
    sums = [None, None]
    base = jnp.zeros(kind.shape, f32)
    for s in range(kinds):
        total = jnp.sum(lowest_ref[s] * weights_ref[...], axis=1, keepdims=True)
        for z in range(2):
            value = jnp.broadcast_to(total[1 - z : 2 - z], kind.shape)
            sums[z] = value if s == 0 else jnp.where(kind == s, value, sums[z])
        base = jnp.where(kind == s, valence_ref[s], base)
    base = jnp.where(energy == 0, base, jnp.zeros_like(base))

    hear(0)
    tell(1)
    halos[0].wait_recv()
    products(0, halo_ref.at[0])
    c_ref[...] += plane_sum(nbr_ref, gx_ref, l_refs[0], *ends[0], dirs, range(PLANE))
    hear(1)
    tell(2)
    halos[1].wait_recv()
    products(2, halo_ref.at[1])
    for index in range(2, rounds):
        hear(index)
        tell(index + 1)

    for part in range(PARTS):
        atoms = range(part * PLANE // PARTS, (part + 1) * PLANE // PARTS)
        rows = pl.ds(atoms[0] * order, len(atoms) * order)
        total = c_ref[rows, :] + plane_sum(nbr_ref, gx_ref, l_refs[2], *ends[2], dirs, atoms)
        series(tile_ref.at[1], total, wd_ref, v_ref, atoms, order)
    projected = project(table_ref, v_ref, order)
    store_scaled(projected, w_ref[0, 0], w_ref[0, 1], mine_ref)

    q = mine_ref[0, :, 0:1] * sums[0] + mine_ref[1, :, 0:1] * sums[1] - base
    row = lax.broadcasted_iota(jnp.int32, (PLANE, LANES), 0)
    lane = lax.broadcasted_iota(jnp.int32, (PLANE, LANES), 1)
    spot = lane == row + PLANE * lax.rem(atom, LANES // PLANE)
    q_ref[me] = jnp.sum(jnp.where(spot, q, jnp.zeros((PLANE, LANES), f32)), axis=0, keepdims=True)
    hear(rounds)

    def spread(ahead_by):
        place = lax.rem(atom + ahead_by, ring)
        for step in range(energies):
            if isinstance(ahead_by, int) and ahead_by == 0 and step == 0:
                continue
            pltpu.make_async_remote_copy(
                src_ref=q_ref.at[me], dst_ref=q_ref.at[me], send_sem=q_send, recv_sem=q_recv,
                device_id={"atom": place, "energy": lax.rem(energy + step, energies)}, device_id_type=MESH,
            ).start()

    if ring <= 2 * PLANE:
        for ahead_by in sorted(range(1, ring), key=lambda d: -min(d, ring - d)):
            spread(ahead_by)
    else:
        lax.fori_loop(1, ring, lambda d, carry: (spread(d), carry)[1], 0)
    spread(0)
    coefs = []
    for step in range(1, energies):
        copy = pltpu.make_async_remote_copy(
            src_ref=mine_ref, dst_ref=coef_ref.at[energy], send_sem=coef_send.at[step],
            recv_sem=coef_recv.at[step], device_id=peer(step), device_id_type=MESH,
        )
        copy.start()
        coefs.append(copy)
    coef_ref[energy] = mine_ref[...]

    keep.wait()
    loads[10].wait()
    for copy in pieces + coefs:
        copy.wait()
    density_of(kind, coef_ref, pieces_ref, old_ref, density_ref, potential_ref)
    for copy in halos:
        copy.wait_send()
    rest = q_ref.at[pl.ds(0, devices - 1)]
    pltpu.make_async_copy(rest, rest, q_send).wait()
    pltpu.make_async_copy(rest, rest, q_recv).wait()
    group = LANES // PLANE * energies
    shift = jnp.zeros((PLANE, 1), f32)
    for g in range(ring * PLANE // LANES):
        charges = jnp.sum(q_ref[pl.ds(g * group, group), 0, :], axis=0, keepdims=True)
        shift = shift + jnp.sum(madelung_ref[:, pl.ds(g * LANES, LANES)] * charges, axis=1, keepdims=True)
    potential_ref[0] = (1.0 - mixing) * old_ref[0] + mixing * (density_ref[0] + shift)


def core_scratch(order, dirs, ring, energies, channels, kinds, width):
    dma = pltpu.SemaphoreType.DMA
    return [
        pltpu.SMEM((PLANE, dirs), jnp.int32),
        pltpu.SMEM((1, 2), f32),
        pltpu.SMEM((kinds,), f32),
        pltpu.VMEM((PLANE, 2 * ROWS, LANES), f32),
        pltpu.VMEM((dirs, 2 * ROWS, LANES), f32),
        pltpu.VMEM((channels, order * order), f32),
        pltpu.VMEM((kinds, 2, width * energies), f32),
        pltpu.VMEM((1, width * energies), f32),
        pltpu.VMEM((1, PLANE), jnp.int32),
        pltpu.VMEM((PLANE, ring * PLANE), f32),
        pltpu.VMEM((channels, PLANE, width), f32),
        pltpu.VMEM((energies, kinds, channels, 2, width), f32),
        pltpu.VMEM((energies, 2, PLANE, channels), f32),
        pltpu.VMEM((2, PLANE, channels), f32),
        pltpu.VMEM((ring * energies, 1, LANES), f32),
        pltpu.VMEM((2, PLANE, 2 * ROWS, LANES), f32),
        pltpu.VMEM((dirs // 2, order, LANES), f32),
        pltpu.VMEM((3, PLANE // 2, order, LANES), f32),
        pltpu.VMEM((dirs, 2 * order, LANES), bf16),
        *(pltpu.VMEM((stop - start, PLANE, order, LANES), bf16) for start, stop in ends_of(dirs)),
        pltpu.VMEM((PLANE * order, LANES), f32),
        pltpu.VMEM((PLANE // 2, LANES, 2 * LANES), bf16),
        pltpu.VMEM((LANES, order * order), bf16),
        pltpu.VMEM((PLANE // 2 * order, LANES), f32),
        dma((11,)), dma, dma((2,)), dma((2,)), dma((energies,)), dma((energies,)), dma((energies,)),
        dma((energies,)), dma, dma, pltpu.SemaphoreType.REGULAR((far_rounds(ring) + 1,)),
    ]


def emit(density_ref, potential_ref, density_out, potential_out, sems):
    channels = density_ref.shape[0]
    edges = [channels * i // CHUNKS for i in range(CHUNKS + 1)]
    copies = []
    for i in range(CHUNKS):
        part = pl.ds(edges[i], edges[i + 1] - edges[i])
        for j, (src, dst) in enumerate(((density_ref, density_out), (potential_ref, potential_out))):
            copies.append(pltpu.make_async_copy(src.at[part], dst.at[part], sems.at[2 * i + j]))
            copies[-1].start()
    for copy in copies:
        copy.wait()


VMEM = pl.BlockSpec(memory_space=pltpu.VMEM)
ANY = pl.BlockSpec(memory_space=pl.ANY)
HBM = pl.BlockSpec(memory_space=pltpu.HBM)
MESH = pl.DeviceIdType.MESH


def shards(single_site, structure, neighbours, species, valence, energy_weights, gaunt_table,
           radial_shapes, radial_weights, madelung, old_potential):
    atom_rows, energy_rows = single_site.shape[:2]
    dirs = structure.shape[1]
    order = int(round(single_site.shape[3] ** 0.5))
    channels, width = old_potential.shape[1], old_potential.shape[2]
    kinds = radial_shapes.shape[0]
    energies = lax.axis_size("energy")
    assert atom_rows == PLANE and energy_rows == 1 and order == 32 and channels <= 64

    def parts(x):
        x = x.reshape(-1, 2, order * order // LANES, LANES)
        return jnp.transpose(x, (0, 2, 1, 3)).reshape(-1, 2 * ROWS, LANES)

    shapes = jnp.transpose(radial_shapes[:, 0], (0, 2, 1, 3))
    ring = lax.axis_size("atom")
    whole = [jax.ShapeDtypeStruct((channels, atom_rows, width), f32)] * 2
    operands = (neighbours, energy_weights, valence, parts(single_site), parts(structure), gaunt_table, shapes,
                radial_weights[None, :], species[None, :], madelung, jnp.transpose(old_potential, (1, 0, 2)))
    density, potential = pl.pallas_call(
        functools.partial(core, order, dirs, ring, energies),
        out_shape=whole,
        in_specs=[HBM] * 11,
        out_specs=[VMEM] * 2,
        scratch_shapes=core_scratch(order, dirs, ring, energies, channels, kinds, width),
        compiler_params=pltpu.CompilerParams(
            collective_id=0, has_side_effects=True, vmem_limit_bytes=32 * 1024 * 1024
        ),
        name="scatter",
    )(*(pltpu.with_memory_space_constraint(x, pltpu.HBM) for x in operands))
    density, potential = pl.pallas_call(
        emit,
        out_shape=whole,
        in_specs=[ANY] * 2,
        out_specs=[ANY] * 2,
        scratch_shapes=[pltpu.SemaphoreType.DMA((2 * CHUNKS,))],
        compiler_params=pltpu.CompilerParams(vmem_limit_bytes=1024 * 1024),
        name="emit",
    )(density, potential)

    back = lambda x: jnp.transpose(x, (1, 0, 2))
    return back(density), back(potential)


def solution(mesh):
    in_specs = (
        P("atom", "energy", None, None),
        P("energy", None, None, None),
        P("atom", None),
        P("atom"),
        P(),
        P("energy", None),
        P(),
        P(None, "energy", None, None, None),
        P(),
        P("atom", None),
        P("atom", None, "energy"),
    )
    out_specs = (P("atom", None, "energy"), P("atom", None, "energy"))
    return jax.shard_map(shards, mesh=mesh, in_specs=in_specs, out_specs=out_specs, check_vma=False)
```
